512 devices in a mesh: dp: 64 (over z, y_hi, core), own: 8 (over y_lo, x).
Axes of the slice: x: 4, y: 8 (y_hi: 4, y_lo: 2; y = y_hi * 2 + y_lo), z: 8, core: 2. Of those that a mesh axis runs over, the one named last changes fastest.
Arguments:
- wide_rows: bfloat16 [8, 393216, 256], P(None, ('dp', 'own'))
- narrow_rows: bfloat16 [8, 393216, 128], P(None, ('dp', 'own'))
- owner_map: int32 [8], replicated, may hold values from 0 to 7, as said below
Outputs:
- kept_inverse: float32 [16, 256, 256], P('own', None, 'dp')
- update: float32 [8, 128, 256], P(None, 'own', 'dp')
The draws below stay inside these ranges and needn't reach their ends.
Inputs may be any that keep to these rules, and one draw needn't show every extreme that they name: owner_map[l] names the owner of layer l; no owner has more than 2 layers, and one owner has exactly 2.
All inputs are finite; a program needn't handle non-finite values.
Results may differ from the reference program's by a relative error of at most 0.0003.
Values sent between devices are 32-bit elements; how exact they have to be, the bound alone decides.
A program may use at most 64 MiB of HBM per device.

```python
import jax
import jax.numpy as jnp
from jax import lax

WIDE = 256
NARROW = 128
LAYERS = 8
ROWS_DEV = 768
CAP = 2
ROWS = 393216
SLOTS = 16
N_OWN = 8


def base_noise(key, shape):
    return jax.random.normal(key, shape, jnp.float32)


def shaped_rows(key, raw, width):
    row_ids = jnp.arange(ROWS, dtype=jnp.int32)
    frac = row_ids.astype(jnp.float32) / ROWS
    scale = jnp.exp(jnp.log(3.0) * (frac - 0.5))
    mixed = raw + 0.7 * jnp.roll(raw, 1, axis=2) - 0.5 * jnp.roll(raw, 7, axis=2)
    device = row_ids // ROWS_DEV
    column = jnp.arange(width, dtype=jnp.int32)
    boost = 1.0 + 2.0 * (column[None, :] == (device % width)[:, None]).astype(jnp.float32)
    column_draw = jax.random.uniform(jax.random.fold_in(key, 37), (LAYERS, 1, width), jnp.float32, 0.0, 1.0)
    column_scale = 4.0 * jnp.exp(jnp.log(10.0) * (column_draw - 0.5))
    return mixed * scale[None, :, None] * boost[None, :, :] * column_scale


def draw_wide_rows(key, part):
    raw = base_noise(jax.random.fold_in(key, 11), (LAYERS, ROWS, WIDE))
    return shaped_rows(jax.random.fold_in(key, 13), raw, WIDE).astype(jnp.bfloat16)


def draw_narrow_rows(key, part):
    shared = base_noise(jax.random.fold_in(key, 11), (LAYERS, ROWS, WIDE))
    own_part = base_noise(jax.random.fold_in(key, 12), (LAYERS, ROWS, NARROW))
    raw = own_part + 0.8 * shared[:, :, :NARROW]
    return shaped_rows(jax.random.fold_in(key, 14), raw, NARROW).astype(jnp.bfloat16)


def draw_owner_map(key, part):
    first = jax.random.randint(jax.random.fold_in(key, 21), (), 0, N_OWN)
    layer_order = jax.random.permutation(jax.random.fold_in(key, 22), LAYERS)
    other_slots = jax.random.permutation(jax.random.fold_in(key, 23), (N_OWN - 1) * CAP)
    ranks = jnp.arange(LAYERS, dtype=jnp.int32)
    picked = other_slots[jnp.clip(ranks - CAP, 0, (N_OWN - 1) * CAP - 1)]
    others = (first + 1 + picked // CAP) % N_OWN
    owners = jnp.where(ranks < CAP, first, others).astype(jnp.int32)
    result = jnp.zeros((LAYERS,), jnp.int32).at[layer_order].set(owners)
    return result


def setup_inputs(seed: int = 0) -> dict:
    keys = jax.random.split(jax.random.key(seed), 4)
    wide_rows = draw_wide_rows(jax.random.fold_in(keys[3], 71), 0)
    narrow_rows = draw_narrow_rows(jax.random.fold_in(keys[3], 71), 0)
    owner_map = draw_owner_map(jax.random.fold_in(keys[3], 71), 0)
    return {"wide_rows": wide_rows, "narrow_rows": narrow_rows, "owner_map": owner_map}


DAMP = 0.5

def layer_stats(pair):
    wide, narrow = pair
    wcov = jnp.dot(wide.T.astype(jnp.float32), wide.astype(jnp.float32), preferred_element_type=jnp.float32)
    ncov = jnp.dot(narrow.T.astype(jnp.float32), narrow.astype(jnp.float32), preferred_element_type=jnp.float32)
    mixed = jnp.dot(narrow.T.astype(jnp.float32), wide.astype(jnp.float32), preferred_element_type=jnp.float32)
    return (wcov, ncov, mixed)

def solve_with(factor, rhs):
    return jax.scipy.linalg.cho_solve((factor, True), rhs)

def reference(wide_rows, narrow_rows, owner_map):
    wcov, ncov, mixed = lax.map(layer_stats, (wide_rows, narrow_rows))
    wcov = wcov / ROWS
    ncov = ncov / ROWS
    mixed = mixed / ROWS
    wide_eye = jnp.eye(WIDE, dtype=jnp.float32)
    narrow_eye = jnp.eye(NARROW, dtype=jnp.float32)
    wchol = jax.vmap(jnp.linalg.cholesky)(wcov + DAMP * wide_eye)
    nchol = jax.vmap(jnp.linalg.cholesky)(ncov + DAMP * narrow_eye)
    winv = jax.vmap(lambda c: solve_with(c, wide_eye))(wchol)
    inner = jnp.einsum('lnw,lwk->lnk', mixed, winv, precision=lax.Precision.HIGHEST)
    update = jax.vmap(solve_with)(nchol, inner)
    same = owner_map[:, None] == owner_map[None, :]
    order = jnp.arange(LAYERS, dtype=jnp.int32)
    earlier = order[None, :] < order[:, None]
    rank = jnp.sum((same & earlier).astype(jnp.int32), axis=1)
    slot = (owner_map * CAP + rank).astype(jnp.int32)
    kept = jnp.broadcast_to(wide_eye / DAMP, (SLOTS, WIDE, WIDE))
    kept = kept.at[slot].set(winv)
    return (kept, update)
```

```python
import functools

import jax
import jax.numpy as jnp
from jax import lax
from jax.experimental import pallas as pl
from jax.experimental.pallas import tpu as pltpu
from jax.sharding import PartitionSpec as P

DAMP = 0.5
MESH = pl.DeviceIdType.MESH
HI = lax.Precision.HIGHEST
f32, bf16 = jnp.float32, jnp.bfloat16
LAYERS, ROWS, WIDE, NARROW = 8, 768, 256, 128
NZ, NY, NO = 8, 4, 8
HALF = 384
ZROWS = HALF // NZ


def place():
    dp = lax.axis_index("dp")
    return dp, lax.axis_index("own"), dp // 8, lax.rem(dp // 2, 4), lax.rem(dp, 2)


def remote(src, dst, send, recv, dp, own):
    return pltpu.make_async_remote_copy(
        src_ref=src, dst_ref=dst, send_sem=send, recv_sem=recv,
        device_id=(dp, own), device_id_type=MESH,
    )


def gram(a, b):
    return lax.dot_general(a, b, (((0,), (0,)), ((), ())), preferred_element_type=f32)


def sum_kernel(
    wide_hbm, narrow_hbm, out_ref, wbuf, nbuf, part, core_rx, own_rx, z_rx, y_rx, z_tx, y_tx,
    in_sem, s0, r0, s1, r1, s2, r2, s3, r3, s4, r4, s5, r5,
):
    dp, own, z, yh, core = place()
    sib = dp + 1 - 2 * core

    def layer_of(t):
        return lax.rem(own + 1 + t, LAYERS)

    def loads(t):
        l = layer_of(t)
        return (
            pltpu.make_async_copy(wide_hbm.at[l], wbuf.at[t], in_sem.at[0, t]),
            pltpu.make_async_copy(narrow_hbm.at[l], nbuf.at[t], in_sem.at[1, t]),
        )

    for t in range(LAYERS):
        for copy in loads(t):
            copy.start()

    def z_peer(i):
        zz = lax.rem(z + i, NZ)
        return zz, zz * 8 + yh * 2 + core

    def y_peer(i):
        yy = lax.rem(yh + i, NY)
        return yy, z * 8 + yy * 2 + core

    def own_peer(i):
        return lax.rem(own + i, NO)

    barrier = pltpu.get_barrier_semaphore()
    pl.semaphore_signal(barrier, inc=1, device_id=(sib, own), device_id_type=MESH)
    for i in range(1, NO):
        pl.semaphore_signal(barrier, inc=1, device_id=(dp, own_peer(i)), device_id_type=MESH)
    for i in range(1, NZ):
        pl.semaphore_signal(barrier, inc=1, device_id=(z_peer(i)[1], own), device_id_type=MESH)
    for i in range(1, NY):
        pl.semaphore_signal(barrier, inc=1, device_id=(y_peer(i)[1], own), device_id_type=MESH)

    def core_copy(t):
        return remote(part.at[t, 1 - core], core_rx.at[t], s0.at[t], r0.at[t], sib, own)

    def own_copy(t):
        return remote(part.at[t, core], own_rx.at[t], s1.at[t], r1.at[t], dp, layer_of(t))

    def stats(t):
        for copy in loads(t):
            copy.wait()
        wide, narrow = wbuf[t], nbuf[t]
        left, right = wide[:, :128], wide[:, 128:]
        top = gram(left, wide)
        part[t, 0, 0:128, :] = top[:, :128]
        part[t, 0, 128:256, :] = top[:, 128:]
        part[t, 0, 256:384, :] = gram(right, right)
        part[t, 1, 0:128, :] = gram(narrow, narrow)
        mixed = gram(narrow, wide)
        part[t, 1, 128:256, :] = mixed[:, :128]
        part[t, 1, 256:384, :] = mixed[:, 128:]

    def pass_on(t):
        core_copy(t).wait_recv()
        part[t, core] = part[t, core] + core_rx[t]

    stats(0)
    pl.semaphore_wait(barrier, 1 + (NO - 1) + (NZ - 1) + (NY - 1))
    core_copy(0).start()

    @pl.loop(1, LAYERS)
    def _(t):
        stats(t)
        core_copy(t).start()
        pass_on(t - 1)
        own_copy(t - 1).start()

    pass_on(LAYERS - 1)
    for t in range(LAYERS - 1):
        own_copy(t).wait_recv()
    total = part[LAYERS - 1, core]
    for t in range(LAYERS - 1):
        total = total + own_rx[t]
    z_tx[...] = total.reshape(NZ, ZROWS, 128)

    def z_copy(i):
        zz, peer = z_peer(i)
        return remote(z_tx.at[zz], z_rx.at[i], s2.at[i], r2.at[i], peer, own)

    for i in range(1, NZ):
        z_copy(i).start()
    acc = z_tx[z]
    for i in range(1, NZ):
        z_copy(i).wait_recv()
        acc = acc + z_rx[i]
    y_tx[...] = acc

    def y_copy(i):
        return remote(y_tx, y_rx.at[i], s3.at[i], r3.at[i], y_peer(i)[1], own)

    for i in range(1, NY):
        y_copy(i).start()
    acc = y_tx[...]
    for i in range(1, NY):
        y_copy(i).wait_recv()
        acc = acc + y_rx[i]
    out_ref[core, z] = acc

    def gather_copy(i):
        return remote(out_ref.at[core, z], out_ref.at[core, z], s4.at[i], r4.at[i], z_peer(i)[1], own)

    def arrival(i):
        zz = lax.rem(z + NZ - i, NZ)
        return remote(out_ref.at[core, zz], out_ref.at[core, zz], s4.at[i], r4.at[i], z_peer(i)[1], own)

    def twin_copy(i):
        zz = lax.rem(z + NZ - i, NZ)
        return remote(out_ref.at[core, zz], out_ref.at[core, zz], s5.at[i], r5.at[i], sib, own)

    def twin_arrival(i):
        zz = lax.rem(z + NZ - i, NZ)
        return remote(out_ref.at[1 - core, zz], out_ref.at[1 - core, zz], s5.at[i], r5.at[i], sib, own)

    for i in range(1, NZ):
        gather_copy(i).start()
    twin_copy(0).start()
    for i in range(1, NZ):
        arrival(i).wait_recv()
        twin_copy(i).start()
    for i in range(NZ):
        twin_arrival(i).wait_recv()

    for t in range(LAYERS):
        core_copy(t).wait_send()
    for t in range(LAYERS - 1):
        own_copy(t).wait_send()
    for i in range(1, NZ):
        z_copy(i).wait_send()
    for i in range(1, NY):
        y_copy(i).wait_send()
    for i in range(1, NZ):
        gather_copy(i).wait_send()
    for i in range(NZ):
        twin_copy(i).wait_send()


def summed_stats(wide_rows, narrow_rows):
    dma = pltpu.SemaphoreType.DMA
    return pl.pallas_call(
        sum_kernel,
        out_shape=jax.ShapeDtypeStruct((2, NZ, ZROWS, 128), f32),
        in_specs=[pl.BlockSpec(memory_space=pl.ANY)] * 2,
        out_specs=pl.BlockSpec(memory_space=pltpu.VMEM),
        scratch_shapes=[
            pltpu.VMEM((LAYERS, ROWS, WIDE), bf16),
            pltpu.VMEM((LAYERS, ROWS, NARROW), bf16),
            pltpu.VMEM((LAYERS, 2, HALF, 128), f32),
            pltpu.VMEM((LAYERS, HALF, 128), f32),
            pltpu.VMEM((LAYERS - 1, HALF, 128), f32),
            pltpu.VMEM((NZ, ZROWS, 128), f32),
            pltpu.VMEM((NY, ZROWS, 128), f32),
            pltpu.VMEM((NZ, ZROWS, 128), f32),
            pltpu.VMEM((ZROWS, 128), f32),
            dma((2, LAYERS)), dma((LAYERS,)), dma((LAYERS,)), dma((LAYERS,)), dma((LAYERS,)),
            dma((NZ,)), dma((NZ,)), dma((NY,)), dma((NY,)),
            dma((NZ,)), dma((NZ,)), dma((NZ,)), dma((NZ,)),
        ],
        compiler_params=pltpu.CompilerParams(
            collective_id=0, has_side_effects=True, vmem_limit_bytes=40 << 20
        ),
    )(wide_rows, narrow_rows)


def split3(x):
    a = x.astype(bf16)
    r = x - a.astype(f32)
    b = r.astype(bf16)
    r = r - b.astype(f32)
    return a, b, r.astype(bf16)


def outer(p, r):
    p1, p2, p3 = split3(p)
    r1, r2, r3 = split3(r)
    lhs = jnp.concatenate([p1, p1, p2, p2, p1, p3], 0)
    rhs = jnp.concatenate([r1, r2, r1, r2, r3, r1], 0)
    return lax.dot_general(lhs, rhs, (((0,), (0,)), ((), ())), preferred_element_type=f32)


def sweep_panel(a_ref, k, n):
    lo = 8 * k
    sub = lax.broadcasted_iota(jnp.int32, (8, 128), 0)
    lane = lax.broadcasted_iota(jnp.int32, (8, 128), 1)
    rows = a_ref[lo : lo + 8, :]
    chunks = [rows[:, 128 * c : 128 * c + 128] for c in range(n // 128)]
    kc, kl = lo // 128, lo % 128
    cols = [jnp.broadcast_to(chunks[kc][:, kl + j : kl + j + 1], (8, 128)) for j in range(8)]
    for p in range(8):
        rec = 1.0 / jnp.broadcast_to(cols[p][p : p + 1, :], (8, 128))
        factor = cols[p]
        here = sub == p
        unit = jnp.where(here, 1.0, 0.0)
        chunks[kc] = jnp.where(lane == kl + p, unit, chunks[kc])

        def step(x):
            row = jnp.broadcast_to(x[p : p + 1, :], (8, 128)) * rec
            return jnp.where(here, row, x - factor * row)

        chunks = [step(x) for x in chunks]
        cols = [step(cols[j]) if j > p else cols[j] for j in range(8)]
    inside = (lane >= kl) & (lane < kl + 8)
    chunks[kc] = jnp.where(inside, -chunks[kc], chunks[kc])
    swept = jnp.concatenate(chunks, 1) if len(chunks) > 1 else chunks[0]
    change = outer(rows, swept)
    lanes = lax.broadcasted_iota(jnp.int32, (1, n), 1)
    own_cols = (lanes >= lo) & (lanes < lo + 8)
    a_ref[...] = jnp.where(own_cols, 0.0, a_ref[...]) - change
    a_ref[lo : lo + 8, :] = swept


def eye(n):
    i = lax.broadcasted_iota(jnp.int32, (n, n), 0)
    j = lax.broadcasted_iota(jnp.int32, (n, n), 1)
    return jnp.where(i == j, 1.0, 0.0).astype(f32)


def inverse_kernel(total, s_ref, out_ref, a_ref, n_ref):
    dp = lax.axis_index("dp")
    damp = DAMP * eye(128)
    cross = s_ref[128:256, :] / total
    a_ref[0:128, 0:128] = s_ref[0:128, :] / total + damp
    a_ref[0:128, 128:256] = cross
    a_ref[128:256, 0:128] = cross.T
    a_ref[128:256, 128:256] = s_ref[256:384, :] / total + damp
    n_ref[...] = s_ref[384:512, :] / total + damp
    for k in range(WIDE // 8):
        sweep_panel(a_ref, k, WIDE)
        if k < NARROW // 8:
            sweep_panel(n_ref, k, NARROW)
    x = -a_ref[pl.ds(pl.multiple_of(dp // 2 * 8, 8), 8), :]
    last = (((1,), (1,)), ((), ()))
    inner = lax.dot_general(x[:, :128], s_ref[512:640, :] / total, last, precision=HI, preferred_element_type=f32)
    inner = inner + lax.dot_general(x[:, 128:], s_ref[640:768, :] / total, last, precision=HI, preferred_element_type=f32)
    u = -jnp.dot(inner, n_ref[...], precision=HI, preferred_element_type=f32)
    both = jnp.concatenate([x, u], 1)
    out_ref[...] = jnp.where(lax.rem(dp, 2) == 0, both[0:4], both[4:8])


def inverse_columns(stats, total):
    return pl.pallas_call(
        functools.partial(inverse_kernel, float(total)),
        out_shape=jax.ShapeDtypeStruct((4, WIDE + NARROW), f32),
        in_specs=[pl.BlockSpec(memory_space=pltpu.VMEM)],
        out_specs=pl.BlockSpec(memory_space=pltpu.VMEM),
        scratch_shapes=[pltpu.VMEM((WIDE, WIDE), f32), pltpu.VMEM((NARROW, NARROW), f32)],
    )(stats)


def exchange_kernel(cols_ref, table_ref, kept_ref, update_ref, rx, send, recv):
    dp, own, _, _, _ = place()

    def peer(i):
        return lax.rem(own + i, NO)

    barrier = pltpu.get_barrier_semaphore()
    for i in range(1, NO):
        pl.semaphore_signal(barrier, inc=1, device_id=(dp, peer(i)), device_id_type=MESH)
    pl.semaphore_wait(barrier, NO - 1)

    def copy(i):
        return remote(cols_ref, rx.at[own], send.at[i], recv.at[i], dp, peer(i))

    def arrival(i):
        return remote(cols_ref, rx.at[lax.rem(own + NO - i, NO)], send.at[i], recv.at[i], dp, peer(i))

    for i in range(1, NO):
        copy(i).start()
    rx[own] = cols_ref[...]
    i0 = lax.broadcasted_iota(jnp.int32, (4, WIDE), 0)
    i1 = lax.broadcasted_iota(jnp.int32, (4, WIDE), 1)
    empty = jnp.where(i1 == dp * 4 + i0, 1.0 / DAMP, 0.0).astype(f32)
    for i in range(1, NO):
        arrival(i).wait_recv()
    kept = [empty, empty]
    shift = lax.rem(128 - 16 * own, 128)
    for l in range(LAYERS):
        got = rx[l]
        for c in range(2):
            hit = jnp.broadcast_to(table_ref[c, l : l + 1, 0:1], (4, WIDE)) > 0.5
            kept[c] = jnp.where(hit, got[:, :WIDE], kept[c])
        part = jnp.concatenate([got[:, WIDE:], got[:, WIDE:]], 0)
        update_ref[l] = pltpu.roll(part, shift, 1)[0:4, 0:16]
    kept_ref[0] = kept[0]
    kept_ref[1] = kept[1]
    for i in range(1, NO):
        copy(i).wait_send()


def exchange(cols, table):
    dma = pltpu.SemaphoreType.DMA
    vmem = pl.BlockSpec(memory_space=pltpu.VMEM)
    return pl.pallas_call(
        exchange_kernel,
        out_shape=(
            jax.ShapeDtypeStruct((2, 4, WIDE), f32),
            jax.ShapeDtypeStruct((LAYERS, 4, 16), f32),
        ),
        in_specs=[vmem, vmem],
        out_specs=(vmem, vmem),
        scratch_shapes=[pltpu.VMEM((NO, 4, WIDE + NARROW), f32), dma((NO,)), dma((NO,))],
        compiler_params=pltpu.CompilerParams(collective_id=1, has_side_effects=True),
    )(cols, table)


def on_device(wide_rows, narrow_rows, owner_map):
    same = owner_map[:, None] == owner_map[None, :]
    order = jnp.arange(LAYERS, dtype=jnp.int32)
    rank = jnp.sum((same & (order[None, :] < order[:, None])).astype(jnp.int32), axis=1)
    mine = lax.axis_index("own") * 2 + jnp.arange(2, dtype=jnp.int32)
    table = ((owner_map * 2 + rank)[None, :] == mine[:, None]).astype(f32)
    table = jnp.broadcast_to(table[:, :, None], (2, LAYERS, 128))
    stats = summed_stats(wide_rows, narrow_rows).reshape(768, 128)
    cols = inverse_columns(stats, ROWS * 512)
    kept, update = exchange(cols, table)
    return kept.transpose(0, 2, 1), update.transpose(0, 2, 1)


def solution(mesh):
    in_specs = (P(None, ("dp", "own"), None), P(None, ("dp", "own"), None), P())
    out_specs = (P("own", None, "dp"), P(None, "own", "dp"))
    return jax.shard_map(
        on_device, mesh=mesh, in_specs=in_specs, out_specs=out_specs, check_vma=False
    )
```

```python
import functools

import jax
import jax.numpy as jnp
from jax import lax
from jax.experimental import pallas as pl
from jax.experimental.pallas import tpu as pltpu
from jax.sharding import PartitionSpec as P

DAMP = 0.5
MESH = pl.DeviceIdType.MESH
HI = lax.Precision.HIGHEST
f32, bf16 = jnp.float32, jnp.bfloat16
LAYERS, ROWS, WIDE, NARROW = 8, 768, 256, 128
NZ, NY, NO = 8, 4, 8


def place():
    dp = lax.axis_index("dp")
    return dp, lax.axis_index("own"), dp // 8, lax.rem(dp // 2, 4), lax.rem(dp, 2)


def remote(src, dst, send, recv, dp, own):
    return pltpu.make_async_remote_copy(
        src_ref=src, dst_ref=dst, send_sem=send, recv_sem=recv,
        device_id=(dp, own), device_id_type=MESH,
    )


def gram(a, b):
    return lax.dot_general(a, b, (((0,), (0,)), ((), ())), preferred_element_type=f32)


class Stream:
    def __init__(self, refs):
        (self.part, self.core_rx, self.own_rx, self.z_tx, self.z_rx, self.y_tx, self.y_rx, self.fin,
         self.sems, self.sems_y) = refs
        self.dp, self.own, self.z, self.yh, self.core = place()
        self.sib = self.dp + 1 - 2 * self.core

    @staticmethod
    def scratch(rows):
        vmem, dma = pltpu.VMEM, pltpu.SemaphoreType.DMA
        return [
            vmem((LAYERS, 2, rows, 128), f32), vmem((LAYERS, rows, 128), f32),
            vmem((LAYERS - 1, rows, 128), f32), vmem((NZ, rows // NZ, 128), f32),
            vmem((NZ, rows // NZ, 128), f32), vmem((rows // NZ, 128), f32),
            vmem((NY, rows // NZ, 128), f32), vmem((2, NZ, rows // NZ, 128), f32),
            dma((5, 2, 8)), dma((2, NY)),
        ]

    def to(self, src, dst, phase, i, dp, own):
        return remote(src, dst, self.sems.at[phase, 0, i], self.sems.at[phase, 1, i], dp, own)

    def layer_of(self, t):
        return lax.rem(self.own + 1 + t, LAYERS)

    def z_peer(self, i):
        zz = lax.rem(self.z + i, NZ)
        return zz, zz * 8 + self.yh * 2 + self.core

    def y_peer(self, i):
        return self.z * 8 + lax.rem(self.yh + i, NY) * 2 + self.core

    def core_copy(self, t):
        return self.to(self.part.at[t, 1 - self.core], self.core_rx.at[t], 0, t, self.sib, self.own)

    def own_copy(self, t):
        return self.to(self.part.at[t, self.core], self.own_rx.at[t], 1, t, self.dp, self.layer_of(t))

    def pass_on(self, t):
        self.core_copy(t).wait_recv()
        self.part[t, self.core] = self.part[t, self.core] + self.core_rx[t]

    def z_copy(self, i):
        zz, peer = self.z_peer(i)
        return self.to(self.z_tx.at[zz], self.z_rx.at[i], 2, i, peer, self.own)

    def y_copy(self, i):
        return remote(self.y_tx, self.y_rx.at[i], self.sems_y.at[0, i], self.sems_y.at[1, i], self.y_peer(i), self.own)

    def gather_copy(self, i):
        block = self.fin.at[self.core, self.z]
        return self.to(block, block, 3, i, self.z_peer(i)[1], self.own)

    def from_z(self, core, i):
        return self.fin.at[core, lax.rem(self.z + NZ - i, NZ)]

    def arrival(self, i):
        block = self.from_z(self.core, i)
        return self.to(block, block, 3, i, self.z_peer(i)[1], self.own)

    def twin_copy(self, i):
        block = self.from_z(self.core, i)
        return self.to(block, block, 4, i, self.sib, self.own)

    def twin_arrival(self, i):
        block = self.from_z(1 - self.core, i)
        return self.to(block, block, 4, i, self.sib, self.own)

    def own_done(self):
        total = self.part[LAYERS - 1, self.core]
        for t in range(LAYERS - 1):
            self.own_copy(t).wait_recv()
            total = total + self.own_rx[t]
        self.z_tx[...] = total.reshape(self.z_tx.shape)
        for i in range(1, NZ):
            self.z_copy(i).start()

    def z_done(self):
        acc = self.z_tx[self.z]
        for i in range(1, NZ):
            self.z_copy(i).wait_recv()
            acc = acc + self.z_rx[i]
        self.y_tx[...] = acc
        for i in range(1, NY):
            self.y_copy(i).start()

    def y_done(self):
        acc = self.y_tx[...]
        for i in range(1, NY):
            self.y_copy(i).wait_recv()
            acc = acc + self.y_rx[i]
        self.fin[self.core, self.z] = acc
        for i in range(1, NZ):
            self.gather_copy(i).start()
        self.twin_copy(0).start()

    def gather_done(self):
        for i in range(1, NZ):
            self.arrival(i).wait_recv()
            self.twin_copy(i).start()

    def twin_done(self):
        for i in range(NZ):
            self.twin_arrival(i).wait_recv()

    def drain(self):
        for t in range(LAYERS):
            self.core_copy(t).wait_send()
        for t in range(LAYERS - 1):
            self.own_copy(t).wait_send()
        for i in range(1, NZ):
            self.z_copy(i).wait_send()
            self.gather_copy(i).wait_send()
        for i in range(1, NY):
            self.y_copy(i).wait_send()
        for i in range(NZ):
            self.twin_copy(i).wait_send()


def split3(x):
    a = x.astype(bf16)
    r = x - a.astype(f32)
    b = r.astype(bf16)
    r = r - b.astype(f32)
    return a, b, r.astype(bf16)


def outer(p, r):
    p1, p2, p3 = split3(p)
    r1, r2, r3 = split3(r)
    lhs = jnp.concatenate([p1, p1, p2, p2, p1, p3], 0)
    rhs = jnp.concatenate([r1, r2, r1, r2, r3, r1], 0)
    return lax.dot_general(lhs, rhs, (((0,), (0,)), ((), ())), preferred_element_type=f32)


def sweep_panel(a_ref, k, n):
    lo = 8 * k
    sub = lax.broadcasted_iota(jnp.int32, (8, 128), 0)
    lane = lax.broadcasted_iota(jnp.int32, (8, 128), 1)
    rows = a_ref[lo : lo + 8, :]
    chunks = [rows[:, 128 * c : 128 * c + 128] for c in range(n // 128)]
    kc, kl = lo // 128, lo % 128
    cols = [jnp.broadcast_to(chunks[kc][:, kl + j : kl + j + 1], (8, 128)) for j in range(8)]
    for p in range(8):
        rec = 1.0 / jnp.broadcast_to(cols[p][p : p + 1, :], (8, 128))
        factor = cols[p]
        here = sub == p
        unit = jnp.where(here, 1.0, 0.0)
        chunks[kc] = jnp.where(lane == kl + p, unit, chunks[kc])

        def step(x):
            row = jnp.broadcast_to(x[p : p + 1, :], (8, 128)) * rec
            return jnp.where(here, row, x - factor * row)

        chunks = [step(x) for x in chunks]
        cols = [step(cols[j]) if j > p else cols[j] for j in range(8)]
    inside = (lane >= kl) & (lane < kl + 8)
    chunks[kc] = jnp.where(inside, -chunks[kc], chunks[kc])
    swept = jnp.concatenate(chunks, 1) if len(chunks) > 1 else chunks[0]
    change = outer(rows, swept)
    lanes = lax.broadcasted_iota(jnp.int32, (1, n), 1)
    own_cols = (lanes >= lo) & (lanes < lo + 8)
    a_ref[...] = jnp.where(own_cols, 0.0, a_ref[...]) - change
    a_ref[lo : lo + 8, :] = swept


def eye(n):
    i = lax.broadcasted_iota(jnp.int32, (n, n), 0)
    j = lax.broadcasted_iota(jnp.int32, (n, n), 1)
    return jnp.where(i == j, 1.0, 0.0).astype(f32)


def main_kernel(scale, wide_hbm, narrow_hbm, out_ref, wbuf, nbuf, in_sem, a_ref, n_ref, cols_ref, x_sem, *refs):
    first, second = Stream(refs[:10]), Stream(refs[10:])
    dp, own, z, yh, core = place()

    def loads(t):
        l = first.layer_of(t)
        return (
            pltpu.make_async_copy(wide_hbm.at[l], wbuf.at[t], in_sem.at[0, t]),
            pltpu.make_async_copy(narrow_hbm.at[l], nbuf.at[t], in_sem.at[1, t]),
        )

    for t in range(LAYERS):
        for copy in loads(t):
            copy.start()

    def own_peer(i):
        return lax.rem(own + i, NO)

    barrier = pltpu.get_barrier_semaphore()

    def greet(dp, own):
        pl.semaphore_signal(barrier, inc=1, device_id=(dp, own), device_id_type=MESH)

    greet(first.sib, own)
    for i in range(1, NO):
        greet(dp, own_peer(i))
    for i in range(1, NZ):
        greet(first.z_peer(i)[1], own)
    for i in range(1, NY):
        greet(first.y_peer(i), own)

    def stats_first(t):
        for copy in loads(t):
            copy.wait()
        wide, narrow = wbuf[t], nbuf[t]
        right = wide[:, 128:]
        top = gram(wide[:, :128], wide)
        first.part[t, 0, 0:128, :] = top[:, :128]
        first.part[t, 0, 128:256, :] = top[:, 128:]
        first.part[t, 1, 0:128, :] = gram(right, right)
        first.part[t, 1, 128:256, :] = gram(narrow, narrow)

    def stats_second(t):
        mixed = gram(nbuf[t], wbuf[t])
        second.part[t, 0] = mixed[:, :128]
        second.part[t, 1] = mixed[:, 128:]

    stats_first(0)
    pl.semaphore_wait(barrier, 1 + (NO - 1) + (NZ - 1) + (NY - 1))
    first.core_copy(0).start()

    @pl.loop(1, LAYERS)
    def _(t):
        stats_first(t)
        first.core_copy(t).start()
        first.pass_on(t - 1)
        first.own_copy(t - 1).start()

    stats_second(0)
    second.core_copy(0).start()
    first.pass_on(LAYERS - 1)

    @pl.loop(1, LAYERS)
    def _(t):
        stats_second(t)
        second.core_copy(t).start()
        second.pass_on(t - 1)
        second.own_copy(t - 1).start()

    second.pass_on(LAYERS - 1)
    first.own_done()
    first.z_done()
    first.y_done()
    first.gather_done()
    first.twin_done()
    second.own_done()

    damp = DAMP * eye(128)

    def block(b):
        return first.fin[b // 2, (b % 2) * 4 : (b % 2) * 4 + 4].reshape(128, 128) * scale

    cross = block(1)
    a_ref[0:128, 0:128] = block(0) + damp
    a_ref[0:128, 128:256] = cross
    a_ref[128:256, 0:128] = cross.T
    a_ref[128:256, 128:256] = block(2) + damp
    n_ref[...] = block(3) + damp
    between = {8: second.z_done, 16: second.y_done, 24: second.gather_done}
    for k in range(WIDE // 8):
        if k in between:
            between[k]()
        sweep_panel(a_ref, k, WIDE)
        if k < NARROW // 8:
            sweep_panel(n_ref, k, NARROW)
    second.twin_done()
    x = -a_ref[pl.ds(pl.multiple_of(dp // 2 * 8, 8), 8), :]
    last = (((1,), (1,)), ((), ()))
    inner = 0.0
    for b in range(2):
        half = second.fin[b].reshape(128, 128) * scale
        inner = inner + lax.dot_general(x[:, 128 * b : 128 * b + 128], half, last, precision=HI, preferred_element_type=f32)
    u = -jnp.dot(inner, n_ref[...], precision=HI, preferred_element_type=f32)
    both = jnp.concatenate([x, u], 1)
    cols_ref[...] = jnp.where(core == 0, both[0:4], both[4:8])

    def copy(i):
        return remote(cols_ref, out_ref.at[own], x_sem.at[0, i], x_sem.at[1, i], dp, own_peer(i))

    def arrival(i):
        return remote(cols_ref, out_ref.at[own_peer(NO - i)], x_sem.at[0, i], x_sem.at[1, i], dp, own_peer(i))

    for i in range(1, NO):
        copy(i).start()
    out_ref[own] = cols_ref[...]
    for i in range(1, NO):
        arrival(i).wait_recv()
    first.drain()
    second.drain()
    for i in range(1, NO):
        copy(i).wait_send()


def columns(wide_rows, narrow_rows, total):
    vmem, dma = pltpu.VMEM, pltpu.SemaphoreType.DMA
    return pl.pallas_call(
        functools.partial(main_kernel, 1.0 / total),
        out_shape=jax.ShapeDtypeStruct((NO, 4, WIDE + NARROW), f32),
        in_specs=[pl.BlockSpec(memory_space=pltpu.HBM)] * 2,
        out_specs=pl.BlockSpec(memory_space=pltpu.VMEM),
        scratch_shapes=[
            vmem((LAYERS, ROWS, WIDE), bf16), vmem((LAYERS, ROWS, NARROW), bf16), dma((2, LAYERS)),
            vmem((WIDE, WIDE), f32), vmem((NARROW, NARROW), f32), vmem((4, WIDE + NARROW), f32), dma((2, NO)),
            *Stream.scratch(256), *Stream.scratch(128),
        ],
        compiler_params=pltpu.CompilerParams(
            collective_id=0, has_side_effects=True, vmem_limit_bytes=60 << 20
        ),
    )(wide_rows, narrow_rows)


def select_kernel(owners, cols_ref, kept_ref, update_ref):
    dp, own, _, _, _ = place()
    i0 = lax.broadcasted_iota(jnp.int32, (4, WIDE), 0)
    i1 = lax.broadcasted_iota(jnp.int32, (4, WIDE), 1)
    empty = jnp.where(i1 == dp * 4 + i0, 1.0 / DAMP, 0.0).astype(f32)
    kept = [empty, empty]
    shift = lax.rem(128 - 16 * own, 128)
    for l in range(LAYERS):
        slot = owners[l] * 2
        for j in range(l):
            slot = slot + jnp.where(owners[j] == owners[l], 1, 0)
        got = cols_ref[l]
        kept = [jnp.where(slot == own * 2 + c, got[:, :WIDE], kept[c]) for c in range(2)]
        part = jnp.concatenate([got[:, WIDE:], got[:, WIDE:]], 0)
        update_ref[l] = pltpu.roll(part, shift, 1)[0:4, 0:16]
    kept_ref[0] = kept[0]
    kept_ref[1] = kept[1]


def select(owner_map, cols):
    vmem = pl.BlockSpec(memory_space=pltpu.VMEM)
    return pl.pallas_call(
        select_kernel,
        out_shape=(
            jax.ShapeDtypeStruct((2, 4, WIDE), f32),
            jax.ShapeDtypeStruct((LAYERS, 4, 16), f32),
        ),
        in_specs=[pl.BlockSpec(memory_space=pltpu.SMEM), vmem],
        out_specs=(vmem, vmem),
    )(owner_map, cols)


def on_device(wide_rows, narrow_rows, owner_map):
    cols = columns(wide_rows, narrow_rows, ROWS * 512)
    kept, update = select(owner_map, cols)
    return kept.transpose(0, 2, 1), update.transpose(0, 2, 1)


def solution(mesh):
    in_specs = (P(None, ("dp", "own"), None), P(None, ("dp", "own"), None), P())
    out_specs = (P("own", None, "dp"), P(None, "own", "dp"))
    return jax.shard_map(
        on_device, mesh=mesh, in_specs=in_specs, out_specs=out_specs, check_vma=False
    )
```

```python
import functools

import jax
import jax.numpy as jnp
from jax import lax
from jax.experimental import pallas as pl
from jax.experimental.pallas import tpu as pltpu
from jax.sharding import PartitionSpec as P

DAMP = 0.5
MESH = pl.DeviceIdType.MESH
HI = lax.Precision.HIGHEST
f32, bf16 = jnp.float32, jnp.bfloat16
LAYERS, ROWS, WIDE, NARROW = 8, 768, 256, 128
NZ, NY, NO = 8, 4, 8


def place():
    dp = lax.axis_index("dp")
    return dp, lax.axis_index("own"), dp // 8, lax.rem(dp // 2, 4), lax.rem(dp, 2)


def remote(src, dst, send, recv, dp, own):
    return pltpu.make_async_remote_copy(
        src_ref=src, dst_ref=dst, send_sem=send, recv_sem=recv,
        device_id=(dp, own), device_id_type=MESH,
    )


def gram(a, b):
    return lax.dot_general(a, b, (((0,), (0,)), ((), ())), preferred_element_type=f32)


R = 192
ZR = R // NZ
DX = (2, 2, 1, 1, 3, 3, 0, 0)


class Stream:
    def __init__(self, refs):
        (self.part, self.core_rx, self.relay_rx, self.x_rx, self.yl_rx, self.z_tx, self.z_rx, self.y_tx, self.y_rx,
         self.fin, self.sems, self.sems_y) = refs
        self.dp, self.own, self.z, self.yh, self.core = place()
        self.sib = self.dp + 1 - 2 * self.core
        self.x, self.yl = lax.rem(self.own, 4), self.own // 4

    @staticmethod
    def scratch():
        vmem, dma = pltpu.VMEM, pltpu.SemaphoreType.DMA
        return [
            vmem((LAYERS, 2, R, 128), f32), vmem((LAYERS, R, 128), f32), vmem((4, R // 2, 128), f32),
            vmem((4, R, 128), f32), vmem((R, 128), f32), vmem((NZ, ZR, 128), f32), vmem((NZ, ZR, 128), f32),
            vmem((ZR, 128), f32), vmem((NY, ZR, 128), f32), vmem((2, NZ, ZR, 128), f32),
            dma((6, 2, 8)), dma((2, NY)),
        ]

    def to(self, src, dst, phase, i, dp, own):
        return remote(src, dst, self.sems.at[phase, 0, i], self.sems.at[phase, 1, i], dp, own)

    def x_peer(self, d):
        return self.yl * 4 + lax.rem(self.x + d, 4)

    def yl_peer(self):
        return (1 - self.yl) * 4 + self.x

    def layer_of(self, t):
        return (self.yl if t % 2 else 1 - self.yl) * 4 + lax.rem(self.x + DX[t], 4)

    def z_peer(self, i):
        zz = lax.rem(self.z + i, NZ)
        return zz, zz * 8 + self.yh * 2 + self.core

    def y_peer(self, i):
        return self.z * 8 + lax.rem(self.yh + i, NY) * 2 + self.core

    def mine(self, t):
        return self.part.at[t, self.core]

    def core_copy(self, t):
        return self.to(self.part.at[t, 1 - self.core], self.core_rx.at[t], 0, t, self.sib, self.own)

    def relay(self, i):
        half = pl.ds(0, R // 2) if i < 2 else pl.ds(R // 2, R // 2)
        return self.to(
            self.part.at[i % 2, self.core, half], self.relay_rx.at[i], 1, i, self.dp, self.x_peer(1 if i < 2 else 3)
        )

    def x_copy(self, i):
        return self.to(self.mine(i + 2), self.x_rx.at[i], 2, i, self.dp, self.x_peer(1 if i < 2 else 3))

    def yl_copy(self):
        return self.to(self.mine(6), self.yl_rx, 2, 4, self.dp, self.yl_peer())

    def pass_on(self, t):
        self.core_copy(t).wait_recv()
        total = self.part[t, self.core] + self.core_rx[t]
        if t < 2:
            self.part[t, self.core] = total
            self.relay(t).start()
            self.relay(t + 2).start()
        elif t < 6:
            i = t - 2
            self.relay(i).wait_recv()
            lo = 0 if i < 2 else R // 2
            self.part[t, self.core] = total
            self.part[t, self.core, lo : lo + R // 2] = total[lo : lo + R // 2] + self.relay_rx[i]
            self.x_copy(i).start()
        else:
            self.part[t, self.core] = total

    def x_sum(self, t):
        total = self.part[t, self.core]
        for i in (t - 6, t - 4):
            self.x_copy(i).wait_recv()
            total = total + self.x_rx[i]
        return total

    def x_done(self):
        self.part[6, self.core] = self.x_sum(6)
        self.yl_copy().start()
        self.part[7, self.core] = self.x_sum(7)

    def yl_done(self):
        self.yl_copy().wait_recv()
        total = self.part[7, self.core] + self.yl_rx[...]
        self.z_tx[...] = total.reshape(NZ, ZR, 128)
        for i in (4, 3, 5, 2, 6, 1, 7):
            self.z_copy(i).start()

    def z_copy(self, i):
        zz, peer = self.z_peer(i)
        return self.to(self.z_tx.at[zz], self.z_rx.at[i], 3, i, peer, self.own)

    def y_copy(self, i):
        return remote(self.y_tx, self.y_rx.at[i], self.sems_y.at[0, i], self.sems_y.at[1, i], self.y_peer(i), self.own)

    def z_done(self):
        acc = self.z_tx[self.z]
        for i in range(1, NZ):
            self.z_copy(i).wait_recv()
            acc = acc + self.z_rx[i]
        self.y_tx[...] = acc
        for i in (2, 1, 3):
            self.y_copy(i).start()

    def gather_copy(self, i):
        block = self.fin.at[self.core, self.z]
        return self.to(block, block, 4, i, self.z_peer(i)[1], self.own)

    def from_z(self, core, i):
        return self.fin.at[core, lax.rem(self.z + NZ - i, NZ)]

    def arrival(self, i):
        block = self.from_z(self.core, i)
        return self.to(block, block, 4, i, self.z_peer(i)[1], self.own)

    def twin_copy(self, i):
        block = self.from_z(self.core, i)
        return self.to(block, block, 5, i, self.sib, self.own)

    def twin_arrival(self, i):
        block = self.from_z(1 - self.core, i)
        return self.to(block, block, 5, i, self.sib, self.own)

    def y_done(self):
        acc = self.y_tx[...]
        for i in range(1, NY):
            self.y_copy(i).wait_recv()
            acc = acc + self.y_rx[i]
        self.fin[self.core, self.z] = acc
        for i in (4, 3, 5, 2, 6, 1, 7):
            self.gather_copy(i).start()
        self.twin_copy(0).start()

    def gather_done(self):
        for i in (1, 7, 2, 6, 3, 5, 4):
            self.arrival(i).wait_recv()
            self.twin_copy(i).start()

    def twin_done(self):
        for i in range(NZ):
            self.twin_arrival(i).wait_recv()

    def drain(self):
        for t in range(LAYERS):
            self.core_copy(t).wait_send()
        for i in range(4):
            self.relay(i).wait_send()
            self.x_copy(i).wait_send()
        self.yl_copy().wait_send()
        for i in range(1, NZ):
            self.z_copy(i).wait_send()
            self.gather_copy(i).wait_send()
        for i in range(1, NY):
            self.y_copy(i).wait_send()
        for i in range(NZ):
            self.twin_copy(i).wait_send()


def split3(x):
    a = x.astype(bf16)
    r = x - a.astype(f32)
    b = r.astype(bf16)
    r = r - b.astype(f32)
    return a, b, r.astype(bf16)


def outer(p, r):
    p1, p2, p3 = split3(p)
    r1, r2, r3 = split3(r)
    lhs = jnp.concatenate([p1, p1, p2, p2, p1, p3], 0)
    rhs = jnp.concatenate([r1, r2, r1, r2, r3, r1], 0)
    return lax.dot_general(lhs, rhs, (((0,), (0,)), ((), ())), preferred_element_type=f32)


class Sweep:
    def __init__(self, ref, n):
        self.ref, self.n, self.ahead = ref, n, None

    def load(self, k):
        rows = self.ref[8 * k : 8 * k + 8, :]
        return [rows[:, 128 * c : 128 * c + 128] for c in range(self.n // 128)]

    def panel(self, k):
        lo, n = 8 * k, self.n
        kc, kl = lo // 128, lo % 128
        sub = lax.broadcasted_iota(jnp.int32, (8, 128), 0)
        lane = lax.broadcasted_iota(jnp.int32, (8, 128), 1)
        chunks = self.load(k) if self.ahead is None else self.ahead
        rows = jnp.concatenate(chunks, 1) if n > 128 else chunks[0]

        def column(x, j):
            return jnp.broadcast_to(x[:, j : j + 1], (8, 128))

        def row(x, j):
            return jnp.broadcast_to(x[j : j + 1, :], (8, 128))

        cols = [column(chunks[kc], kl + j) for j in range(8)]
        more = lo + 8 < n
        if more:
            raw = self.load(k + 1)
            weights = [column(raw[kc], kl + m) for m in range(8)]
        for p in range(8):
            rec = 1.0 / row(cols[p], p)
            factor = cols[p]
            here = sub == p
            chunks = list(chunks)
            chunks[kc] = jnp.where(lane == kl + p, jnp.where(here, 1.0, 0.0), chunks[kc])

            def step(x):
                scaled = row(x, p) * rec
                return jnp.where(here, scaled, x - factor * scaled)

            cols = [step(cols[j]) if j > p else cols[j] for j in range(8)]
            chunks = [step(x) for x in chunks]
        inside = (lane >= kl) & (lane < kl + 8)
        chunks[kc] = jnp.where(inside, -chunks[kc], chunks[kc])
        swept = jnp.concatenate(chunks, 1) if n > 128 else chunks[0]
        if more:
            self.ahead = []
            for c in range(n // 128):
                old = jnp.where(inside, 0.0, raw[c]) if c == kc else raw[c]
                t = [weights[m] * row(chunks[c], m) for m in range(8)]
                self.ahead.append(old - (((t[0] + t[1]) + (t[2] + t[3])) + ((t[4] + t[5]) + (t[6] + t[7]))))
        change = outer(rows, swept)
        lanes = lax.broadcasted_iota(jnp.int32, (1, n), 1)
        own_cols = (lanes >= lo) & (lanes < lo + 8)
        self.ref[...] = jnp.where(own_cols, 0.0, self.ref[...]) - change
        self.ref[lo : lo + 8, :] = swept


def eye(n):
    i = lax.broadcasted_iota(jnp.int32, (n, n), 0)
    j = lax.broadcasted_iota(jnp.int32, (n, n), 1)
    return jnp.where(i == j, 1.0, 0.0).astype(f32)


def main_kernel(scale, wide_hbm, narrow_hbm, out_ref, wbuf, nbuf, in_sem, a_ref, n_ref, cols_ref, x_sem, *refs):
    first, second = Stream(refs[:12]), Stream(refs[12:])
    dp, own, z, yh, core = place()

    def loads(t):
        l = first.layer_of(t)
        return (
            pltpu.make_async_copy(wide_hbm.at[l], wbuf.at[t], in_sem.at[0, t]),
            pltpu.make_async_copy(narrow_hbm.at[l], nbuf.at[t], in_sem.at[1, t]),
        )

    for part in range(2):
        for t in range(LAYERS):
            loads(t)[part].start()

    def own_peer(i):
        return lax.rem(own + i, NO)

    barrier = pltpu.get_barrier_semaphore()

    def greet(dp, own):
        pl.semaphore_signal(barrier, inc=1, device_id=(dp, own), device_id_type=MESH)

    greet(first.sib, own)
    for i in range(1, NO):
        greet(dp, own_peer(i))
    for i in range(1, NZ):
        greet(first.z_peer(i)[1], own)
    for i in range(1, NY):
        greet(first.y_peer(i), own)

    def stats_first(t):
        loads(t)[0].wait()
        wide = wbuf[t]
        right = wide[:, 128:]
        top = gram(wide[:, :128], wide)
        first.part[t, 0, 0:128, :] = top[:, :128]
        first.part[t, 0, 128:192, :] = top[0:64, 128:]
        first.part[t, 1, 0:64, :] = top[64:128, 128:]
        first.part[t, 1, 64:192, :] = gram(right, right)

    def stats_second(t):
        loads(t)[1].wait()
        narrow = nbuf[t]
        mixed = gram(narrow, wbuf[t])
        second.part[t, 0, 0:128, :] = gram(narrow, narrow)
        second.part[t, 0, 128:192, :] = mixed[0:64, :128]
        second.part[t, 1, 0:64, :] = mixed[64:128, :128]
        second.part[t, 1, 64:192, :] = mixed[:, 128:]

    stats_first(0)
    pl.semaphore_wait(barrier, 1 + (NO - 1) + (NZ - 1) + (NY - 1))
    first.core_copy(0).start()
    for t in range(1, LAYERS):
        stats_first(t)
        first.core_copy(t).start()
        first.pass_on(t - 1)
    stats_second(0)
    second.core_copy(0).start()
    first.pass_on(LAYERS - 1)
    for t in range(1, LAYERS):
        stats_second(t)
        second.core_copy(t).start()
        second.pass_on(t - 1)
    second.pass_on(LAYERS - 1)
    first.x_done()
    first.yl_done()
    second.x_done()
    first.z_done()
    second.yl_done()
    first.y_done()
    second.z_done()
    first.gather_done()
    first.twin_done()
    second.y_done()

    damp = DAMP * eye(128)
    wide = first.fin[...].reshape(384, 128) * scale
    cross = wide[128:256]
    a_ref[0:128, 0:128] = wide[0:128] + damp
    a_ref[0:128, 128:256] = cross
    a_ref[128:256, 0:128] = cross.T
    a_ref[128:256, 128:256] = wide[256:384] + damp
    a_sweep, n_sweep = Sweep(a_ref, WIDE), Sweep(n_ref, NARROW)
    late = (WIDE - NARROW) // 8
    for k in range(WIDE // 8):
        a_sweep.panel(k)
        if k == late - 2:
            second.gather_done()
        if k == late - 1:
            second.twin_done()
            n_ref[...] = second.fin[...].reshape(384, 128)[0:128] * scale + damp
        if k >= late:
            n_sweep.panel(k - late)
    x = -a_ref[pl.ds(pl.multiple_of(dp // 2 * 8, 8), 8), :]
    last = (((1,), (1,)), ((), ()))
    mixed = second.fin[...].reshape(384, 128)[128:384] * scale
    inner = 0.0
    for b in range(2):
        half = mixed[128 * b : 128 * b + 128]
        inner = inner + lax.dot_general(x[:, 128 * b : 128 * b + 128], half, last, precision=HI, preferred_element_type=f32)
    u = -jnp.dot(inner, n_ref[...], precision=HI, preferred_element_type=f32)
    both = jnp.concatenate([x, u], 1)
    cols_ref[...] = jnp.where(core == 0, both[0:4], both[4:8])

    def copy(i):
        return remote(cols_ref, out_ref.at[own], x_sem.at[0, i], x_sem.at[1, i], dp, own_peer(i))

    def arrival(i):
        return remote(cols_ref, out_ref.at[own_peer(NO - i)], x_sem.at[0, i], x_sem.at[1, i], dp, own_peer(i))

    for i in range(1, NO):
        copy(i).start()
    out_ref[own] = cols_ref[...]
    first.drain()
    second.drain()
    for i in range(1, NO):
        arrival(i).wait_recv()
    for i in range(1, NO):
        copy(i).wait_send()


def columns(wide_rows, narrow_rows, total):
    vmem, dma = pltpu.VMEM, pltpu.SemaphoreType.DMA
    return pl.pallas_call(
        functools.partial(main_kernel, 1.0 / total),
        out_shape=jax.ShapeDtypeStruct((NO, 4, WIDE + NARROW), f32),
        in_specs=[pl.BlockSpec(memory_space=pltpu.HBM)] * 2,
        out_specs=pl.BlockSpec(memory_space=pltpu.VMEM),
        scratch_shapes=[
            vmem((LAYERS, ROWS, WIDE), bf16), vmem((LAYERS, ROWS, NARROW), bf16), dma((2, LAYERS)),
            vmem((WIDE, WIDE), f32), vmem((NARROW, NARROW), f32), vmem((4, WIDE + NARROW), f32), dma((2, NO)),
            *Stream.scratch(), *Stream.scratch(),
        ],
        compiler_params=pltpu.CompilerParams(
            collective_id=0, has_side_effects=True, vmem_limit_bytes=60 << 20
        ),
    )(wide_rows, narrow_rows)


def select_kernel(owners, cols_ref, kept_ref, update_ref):
    dp, own, _, _, _ = place()
    i0 = lax.broadcasted_iota(jnp.int32, (4, WIDE), 0)
    i1 = lax.broadcasted_iota(jnp.int32, (4, WIDE), 1)
    empty = jnp.where(i1 == dp * 4 + i0, 1.0 / DAMP, 0.0).astype(f32)
    kept = [empty, empty]
    shift = lax.rem(128 - 16 * own, 128)
    for l in range(LAYERS):
        slot = owners[l] * 2
        for j in range(l):
            slot = slot + jnp.where(owners[j] == owners[l], 1, 0)
        got = cols_ref[l]
        kept = [jnp.where(slot == own * 2 + c, got[:, :WIDE], kept[c]) for c in range(2)]
        part = jnp.concatenate([got[:, WIDE:], got[:, WIDE:]], 0)
        update_ref[l] = pltpu.roll(part, shift, 1)[0:4, 0:16]
    kept_ref[0] = kept[0]
    kept_ref[1] = kept[1]


def select(owner_map, cols):
    vmem = pl.BlockSpec(memory_space=pltpu.VMEM)
    return pl.pallas_call(
        select_kernel,
        out_shape=(
            jax.ShapeDtypeStruct((2, 4, WIDE), f32),
            jax.ShapeDtypeStruct((LAYERS, 4, 16), f32),
        ),
        in_specs=[pl.BlockSpec(memory_space=pltpu.SMEM), vmem],
        out_specs=(vmem, vmem),
    )(owner_map, cols)


def on_device(wide_rows, narrow_rows, owner_map):
    cols = columns(wide_rows, narrow_rows, ROWS * 512)
    kept, update = select(owner_map, cols)
    return kept.transpose(0, 2, 1), update.transpose(0, 2, 1)


def solution(mesh):
    in_specs = (P(None, ("dp", "own"), None), P(None, ("dp", "own"), None), P())
    out_specs = (P("own", None, "dp"), P(None, "own", "dp"))
    return jax.shard_map(
        on_device, mesh=mesh, in_specs=in_specs, out_specs=out_specs, check_vma=False
    )
```

```python
import functools

import jax
import jax.numpy as jnp
from jax import lax
from jax.experimental import pallas as pl
from jax.experimental.pallas import tpu as pltpu
from jax.sharding import PartitionSpec as P

DAMP = 0.5
MESH = pl.DeviceIdType.MESH
HI = lax.Precision.HIGHEST
f32, bf16 = jnp.float32, jnp.bfloat16
LAYERS, ROWS, WIDE, NARROW = 8, 768, 256, 128
NZ, NY, NO = 8, 4, 8


def place():
    dp = lax.axis_index("dp")
    return dp, lax.axis_index("own"), dp // 8, lax.rem(dp // 2, 4), lax.rem(dp, 2)


def remote(src, dst, send, recv, dp, own):
    return pltpu.make_async_remote_copy(
        src_ref=src, dst_ref=dst, send_sem=send, recv_sem=recv,
        device_id=(dp, own), device_id_type=MESH,
    )


def gram(a, b):
    return lax.dot_general(a, b, (((0,), (0,)), ((), ())), preferred_element_type=f32)


R = 192
ZR = R // NZ
LAG = 3
DX = (2, 2, 1, 1, 3, 3, 0, 0)


class Stream:
    def __init__(self, refs):
        (self.part, self.core_rx, self.relay_rx, self.x_rx, self.yl_rx, self.z_tx, self.z_rx, self.y_tx, self.y_rx,
         self.fin, self.sems, self.sems_y) = refs
        self.dp, self.own, self.z, self.yh, self.core = place()
        self.sib = self.dp + 1 - 2 * self.core
        self.x, self.yl = lax.rem(self.own, 4), self.own // 4

    @staticmethod
    def scratch():
        vmem, dma = pltpu.VMEM, pltpu.SemaphoreType.DMA
        return [
            vmem((LAYERS, 2, R, 128), f32), vmem((LAYERS, R, 128), f32), vmem((4, R // 2, 128), f32),
            vmem((4, R, 128), f32), vmem((R, 128), f32), vmem((NZ, ZR, 128), f32), vmem((NZ, ZR, 128), f32),
            vmem((ZR, 128), f32), vmem((NY, ZR, 128), f32), vmem((2, NZ, ZR, 128), f32),
            dma((6, 2, 8)), dma((2, NY)),
        ]

    def to(self, src, dst, phase, i, dp, own):
        return remote(src, dst, self.sems.at[phase, 0, i], self.sems.at[phase, 1, i], dp, own)

    def x_peer(self, d):
        return self.yl * 4 + lax.rem(self.x + d, 4)

    def yl_peer(self):
        return (1 - self.yl) * 4 + self.x

    def layer_of(self, t):
        return (self.yl if t % 2 else 1 - self.yl) * 4 + lax.rem(self.x + DX[t], 4)

    def z_peer(self, i):
        zz = lax.rem(self.z + i, NZ)
        return zz, zz * 8 + self.yh * 2 + self.core

    def y_peer(self, i):
        return self.z * 8 + lax.rem(self.yh + i, NY) * 2 + self.core

    def mine(self, t):
        return self.part.at[t, self.core]

    def core_copy(self, t):
        return self.to(self.part.at[t, 1 - self.core], self.core_rx.at[t], 0, t, self.sib, self.own)

    def relay(self, i):
        half = pl.ds(0, R // 2) if i < 2 else pl.ds(R // 2, R // 2)
        return self.to(
            self.part.at[i % 2, self.core, half], self.relay_rx.at[i], 1, i, self.dp, self.x_peer(1 if i < 2 else 3)
        )

    def x_copy(self, i):
        return self.to(self.mine(i + 2), self.x_rx.at[i], 2, i, self.dp, self.x_peer(1 if i < 2 else 3))

    def yl_copy(self):
        return self.to(self.mine(6), self.yl_rx, 2, 4, self.dp, self.yl_peer())

    def pass_on(self, t):
        self.core_copy(t).wait_recv()
        total = self.part[t, self.core] + self.core_rx[t]
        if t < 2:
            self.part[t, self.core] = total
            self.relay(t).start()
            self.relay(t + 2).start()
        elif t < 6:
            i = t - 2
            self.relay(i).wait_recv()
            lo = 0 if i < 2 else R // 2
            self.part[t, self.core] = total
            self.part[t, self.core, lo : lo + R // 2] = total[lo : lo + R // 2] + self.relay_rx[i]
            self.x_copy(i).start()
        else:
            self.part[t, self.core] = total

    def x_sum(self, t):
        total = self.part[t, self.core]
        for i in (t - 6, t - 4):
            self.x_copy(i).wait_recv()
            total = total + self.x_rx[i]
        return total

    def x_done(self):
        self.part[6, self.core] = self.x_sum(6)
        self.yl_copy().start()
        self.part[7, self.core] = self.x_sum(7)

    def yl_done(self):
        self.yl_copy().wait_recv()
        total = self.part[7, self.core] + self.yl_rx[...]
        self.z_tx[...] = total.reshape(NZ, ZR, 128)
        for i in (4, 3, 5, 2, 6, 1, 7):
            self.z_copy(i).start()

    def z_copy(self, i):
        zz, peer = self.z_peer(i)
        return self.to(self.z_tx.at[zz], self.z_rx.at[i], 3, i, peer, self.own)

    def y_copy(self, i):
        return remote(self.y_tx, self.y_rx.at[i], self.sems_y.at[0, i], self.sems_y.at[1, i], self.y_peer(i), self.own)

    def z_done(self):
        acc = self.z_tx[self.z]
        for i in range(1, NZ):
            self.z_copy(i).wait_recv()
            acc = acc + self.z_rx[i]
        self.y_tx[...] = acc
        for i in (2, 1, 3):
            self.y_copy(i).start()

    def gather_copy(self, i):
        block = self.fin.at[self.core, self.z]
        return self.to(block, block, 4, i, self.z_peer(i)[1], self.own)

    def from_z(self, core, i):
        return self.fin.at[core, lax.rem(self.z + NZ - i, NZ)]

    def arrival(self, i):
        block = self.from_z(self.core, i)
        return self.to(block, block, 4, i, self.z_peer(i)[1], self.own)

    def twin_copy(self, i):
        block = self.from_z(self.core, i)
        return self.to(block, block, 5, i, self.sib, self.own)

    def twin_arrival(self, i):
        block = self.from_z(1 - self.core, i)
        return self.to(block, block, 5, i, self.sib, self.own)

    def y_done(self):
        acc = self.y_tx[...]
        for i in range(1, NY):
            self.y_copy(i).wait_recv()
            acc = acc + self.y_rx[i]
        self.fin[self.core, self.z] = acc
        for i in (4, 3, 5, 2, 6, 1, 7):
            self.gather_copy(i).start()
        self.twin_copy(0).start()

    def gather_done(self):
        for i in (1, 7, 2, 6, 3, 5, 4):
            self.arrival(i).wait_recv()
            self.twin_copy(i).start()

    def twin_done(self):
        for i in range(NZ):
            self.twin_arrival(i).wait_recv()

    def drain(self):
        for t in range(LAYERS):
            self.core_copy(t).wait_send()
        for i in range(4):
            self.relay(i).wait_send()
            self.x_copy(i).wait_send()
        self.yl_copy().wait_send()
        for i in range(1, NZ):
            self.z_copy(i).wait_send()
            self.gather_copy(i).wait_send()
        for i in range(1, NY):
            self.y_copy(i).wait_send()
        for i in range(NZ):
            self.twin_copy(i).wait_send()


def split3(x):
    a = x.astype(bf16)
    r = x - a.astype(f32)
    b = r.astype(bf16)
    r = r - b.astype(f32)
    return a, b, r.astype(bf16)


def outer(p, r):
    p1, p2, p3 = split3(p)
    r1, r2, r3 = split3(r)
    lhs = jnp.concatenate([p1, p1, p2, p2, p1, p3], 0)
    rhs = jnp.concatenate([r1, r2, r1, r2, r3, r1], 0)
    return lax.dot_general(lhs, rhs, (((0,), (0,)), ((), ())), preferred_element_type=f32)


class Sweep:
    def __init__(self, ref, n):
        self.ref, self.n, self.ahead = ref, n, None

    def load(self, k):
        rows = self.ref[8 * k : 8 * k + 8, :]
        return [rows[:, 128 * c : 128 * c + 128] for c in range(self.n // 128)]

    def panel(self, k):
        lo, n = 8 * k, self.n
        kc, kl = lo // 128, lo % 128
        sub = lax.broadcasted_iota(jnp.int32, (8, 128), 0)
        lane = lax.broadcasted_iota(jnp.int32, (8, 128), 1)
        chunks = self.load(k) if self.ahead is None else self.ahead
        rows = jnp.concatenate(chunks, 1) if n > 128 else chunks[0]

        def column(x, j):
            return jnp.broadcast_to(x[:, j : j + 1], (8, 128))

        def row(x, j):
            return jnp.broadcast_to(x[j : j + 1, :], (8, 128))

        cols = [column(chunks[kc], kl + j) for j in range(8)]
        more = lo + 8 < n
        if more:
            raw = self.load(k + 1)
            weights = [column(raw[kc], kl + m) for m in range(8)]
        for p in range(8):
            rec = 1.0 / row(cols[p], p)
            factor = cols[p]
            here = sub == p
            chunks = list(chunks)
            chunks[kc] = jnp.where(lane == kl + p, jnp.where(here, 1.0, 0.0), chunks[kc])

            def step(x):
                scaled = row(x, p) * rec
                return jnp.where(here, scaled, x - factor * scaled)

            cols = [step(cols[j]) if j > p else cols[j] for j in range(8)]
            chunks = [step(x) for x in chunks]
        inside = (lane >= kl) & (lane < kl + 8)
        chunks[kc] = jnp.where(inside, -chunks[kc], chunks[kc])
        swept = jnp.concatenate(chunks, 1) if n > 128 else chunks[0]
        if more:
            self.ahead = []
            for c in range(n // 128):
                old = jnp.where(inside, 0.0, raw[c]) if c == kc else raw[c]
                t = [weights[m] * row(chunks[c], m) for m in range(8)]
                self.ahead.append(old - (((t[0] + t[1]) + (t[2] + t[3])) + ((t[4] + t[5]) + (t[6] + t[7]))))
        change = outer(rows, swept)
        lanes = lax.broadcasted_iota(jnp.int32, (1, n), 1)
        own_cols = (lanes >= lo) & (lanes < lo + 8)
        self.ref[...] = jnp.where(own_cols, 0.0, self.ref[...]) - change
        self.ref[lo : lo + 8, :] = swept


def eye(n):
    i = lax.broadcasted_iota(jnp.int32, (n, n), 0)
    j = lax.broadcasted_iota(jnp.int32, (n, n), 1)
    return jnp.where(i == j, 1.0, 0.0).astype(f32)


def main_kernel(scale, wide_hbm, narrow_hbm, out_ref, wbuf, nbuf, in_sem, a_ref, n_ref, cols_ref, x_sem, *refs):
    first, second = Stream(refs[:12]), Stream(refs[12:])
    dp, own, z, yh, core = place()

    def loads(t):
        l = first.layer_of(t)
        return (
            pltpu.make_async_copy(wide_hbm.at[l], wbuf.at[t], in_sem.at[0, t]),
            pltpu.make_async_copy(narrow_hbm.at[l], nbuf.at[t], in_sem.at[1, t]),
        )

    for part in range(2):
        for t in range(LAYERS):
            loads(t)[part].start()

    def own_peer(i):
        return lax.rem(own + i, NO)

    barrier = pltpu.get_barrier_semaphore()

    def greet(dp, own):
        pl.semaphore_signal(barrier, inc=1, device_id=(dp, own), device_id_type=MESH)

    greet(first.sib, own)
    for i in range(1, NO):
        greet(dp, own_peer(i))
    for i in range(1, NZ):
        greet(first.z_peer(i)[1], own)
    for i in range(1, NY):
        greet(first.y_peer(i), own)

    def stats_first(t):
        loads(t)[0].wait()
        wide = wbuf[t]
        right = wide[:, 128:]
        top = gram(wide[:, :128], wide)
        first.part[t, 0, 0:128, :] = top[:, :128]
        first.part[t, 0, 128:192, :] = top[0:64, 128:]
        first.part[t, 1, 0:64, :] = top[64:128, 128:]
        first.part[t, 1, 64:192, :] = gram(right, right)

    def stats_second(t):
        loads(t)[1].wait()
        narrow = nbuf[t]
        mixed = gram(narrow, wbuf[t])
        second.part[t, 0, 0:128, :] = gram(narrow, narrow)
        second.part[t, 0, 128:192, :] = mixed[0:64, :128]
        second.part[t, 1, 0:64, :] = mixed[64:128, :128]
        second.part[t, 1, 64:192, :] = mixed[:, 128:]

    stats_first(0)
    pl.semaphore_wait(barrier, 1 + (NO - 1) + (NZ - 1) + (NY - 1))
    first.core_copy(0).start()
    for t in range(1, LAYERS):
        stats_first(t)
        first.core_copy(t).start()
        if t >= LAG:
            first.pass_on(t - LAG)
    for t in range(LAYERS):
        stats_second(t)
        second.core_copy(t).start()
        if t < LAG:
            first.pass_on(LAYERS - LAG + t)
        else:
            second.pass_on(t - LAG)
    for t in range(LAYERS - LAG, LAYERS):
        second.pass_on(t)
    first.x_done()
    first.yl_done()
    second.x_done()
    second.yl_done()
    first.z_done()
    second.z_done()
    first.y_done()
    first.gather_done()
    first.twin_done()
    second.y_done()

    damp = DAMP * eye(128)
    wide = first.fin[...].reshape(384, 128) * scale
    cross = wide[128:256]
    a_ref[0:128, 0:128] = wide[0:128] + damp
    a_ref[0:128, 128:256] = cross
    a_ref[128:256, 0:128] = cross.T
    a_ref[128:256, 128:256] = wide[256:384] + damp
    a_sweep, n_sweep = Sweep(a_ref, WIDE), Sweep(n_ref, NARROW)
    late = (WIDE - NARROW) // 8
    for k in range(WIDE // 8):
        a_sweep.panel(k)
        if k == late - 2:
            second.gather_done()
        if k == late - 1:
            second.twin_done()
            n_ref[...] = second.fin[...].reshape(384, 128)[0:128] * scale + damp
        if k >= late:
            n_sweep.panel(k - late)
    x = -a_ref[pl.ds(pl.multiple_of(dp // 2 * 8, 8), 8), :]
    last = (((1,), (1,)), ((), ()))
    mixed = second.fin[...].reshape(384, 128)[128:384] * scale
    inner = 0.0
    for b in range(2):
        half = mixed[128 * b : 128 * b + 128]
        inner = inner + lax.dot_general(x[:, 128 * b : 128 * b + 128], half, last, precision=HI, preferred_element_type=f32)
    u = -jnp.dot(inner, n_ref[...], precision=HI, preferred_element_type=f32)
    both = jnp.concatenate([x, u], 1)
    cols_ref[...] = jnp.where(core == 0, both[0:4], both[4:8])

    def copy(i):
        return remote(cols_ref, out_ref.at[own], x_sem.at[0, i], x_sem.at[1, i], dp, own_peer(i))

    def arrival(i):
        return remote(cols_ref, out_ref.at[own_peer(NO - i)], x_sem.at[0, i], x_sem.at[1, i], dp, own_peer(i))

    for i in range(1, NO):
        copy(i).start()
    out_ref[own] = cols_ref[...]
    first.drain()
    second.drain()
    for i in range(1, NO):
        arrival(i).wait_recv()
    for i in range(1, NO):
        copy(i).wait_send()


def columns(wide_rows, narrow_rows, total):
    vmem, dma = pltpu.VMEM, pltpu.SemaphoreType.DMA
    return pl.pallas_call(
        functools.partial(main_kernel, 1.0 / total),
        out_shape=jax.ShapeDtypeStruct((NO, 4, WIDE + NARROW), f32),
        in_specs=[pl.BlockSpec(memory_space=pltpu.HBM)] * 2,
        out_specs=pl.BlockSpec(memory_space=pltpu.VMEM),
        scratch_shapes=[
            vmem((LAYERS, ROWS, WIDE), bf16), vmem((LAYERS, ROWS, NARROW), bf16), dma((2, LAYERS)),
            vmem((WIDE, WIDE), f32), vmem((NARROW, NARROW), f32), vmem((4, WIDE + NARROW), f32), dma((2, NO)),
            *Stream.scratch(), *Stream.scratch(),
        ],
        compiler_params=pltpu.CompilerParams(
            collective_id=0, has_side_effects=True, vmem_limit_bytes=60 << 20
        ),
    )(wide_rows, narrow_rows)


def select_kernel(owners, cols_ref, kept_ref, update_ref):
    dp, own, _, _, _ = place()
    i0 = lax.broadcasted_iota(jnp.int32, (4, WIDE), 0)
    i1 = lax.broadcasted_iota(jnp.int32, (4, WIDE), 1)
    empty = jnp.where(i1 == dp * 4 + i0, 1.0 / DAMP, 0.0).astype(f32)
    kept = [empty, empty]
    shift = lax.rem(128 - 16 * own, 128)
    for l in range(LAYERS):
        slot = owners[l] * 2
        for j in range(l):
            slot = slot + jnp.where(owners[j] == owners[l], 1, 0)
        got = cols_ref[l]
        kept = [jnp.where(slot == own * 2 + c, got[:, :WIDE], kept[c]) for c in range(2)]
        part = jnp.concatenate([got[:, WIDE:], got[:, WIDE:]], 0)
        update_ref[l] = pltpu.roll(part, shift, 1)[0:4, 0:16]
    kept_ref[0] = kept[0]
    kept_ref[1] = kept[1]


def select(owner_map, cols):
    vmem = pl.BlockSpec(memory_space=pltpu.VMEM)
    return pl.pallas_call(
        select_kernel,
        out_shape=(
            jax.ShapeDtypeStruct((2, 4, WIDE), f32),
            jax.ShapeDtypeStruct((LAYERS, 4, 16), f32),
        ),
        in_specs=[pl.BlockSpec(memory_space=pltpu.SMEM), vmem],
        out_specs=(vmem, vmem),
    )(owner_map, cols)


def on_device(wide_rows, narrow_rows, owner_map):
    cols = columns(wide_rows, narrow_rows, ROWS * 512)
    kept, update = select(owner_map, cols)
    return kept.transpose(0, 2, 1), update.transpose(0, 2, 1)


def solution(mesh):
    in_specs = (P(None, ("dp", "own"), None), P(None, ("dp", "own"), None), P())
    out_specs = (P("own", None, "dp"), P(None, "own", "dp"))
    return jax.shard_map(
        on_device, mesh=mesh, in_specs=in_specs, out_specs=out_specs, check_vma=False
    )
```

```python
import functools

import jax
import jax.numpy as jnp
from jax import lax
from jax.experimental import pallas as pl
from jax.experimental.pallas import tpu as pltpu
from jax.sharding import PartitionSpec as P

DAMP = 0.5
MESH = pl.DeviceIdType.MESH
HI = lax.Precision.HIGHEST
f32, bf16 = jnp.float32, jnp.bfloat16
LAYERS, ROWS, WIDE, NARROW = 8, 768, 256, 128
NZ, NY, NO = 8, 4, 8


def place():
    dp = lax.axis_index("dp")
    return dp, lax.axis_index("own"), dp // 8, lax.rem(dp // 2, 4), lax.rem(dp, 2)


def remote(src, dst, send, recv, dp, own):
    return pltpu.make_async_remote_copy(
        src_ref=src, dst_ref=dst, send_sem=send, recv_sem=recv,
        device_id=(dp, own), device_id_type=MESH,
    )


def gram(a, b):
    return lax.dot_general(a, b, (((0,), (0,)), ((), ())), preferred_element_type=f32)


R = 192
ZR = R // NZ
LAG = 4
DX = (2, 2, 1, 1, 3, 3, 0, 0)


class Stream:
    def __init__(self, refs):
        (self.part, self.core_rx, self.relay_rx, self.x_rx, self.yl_rx, self.z_tx, self.z_rx, self.y_tx, self.y_rx,
         self.fin, self.sems, self.sems_y) = refs
        self.dp, self.own, self.z, self.yh, self.core = place()
        self.sib = self.dp + 1 - 2 * self.core
        self.x, self.yl = lax.rem(self.own, 4), self.own // 4

    @staticmethod
    def scratch():
        vmem, dma = pltpu.VMEM, pltpu.SemaphoreType.DMA
        return [
            vmem((LAYERS, 2, R, 128), f32), vmem((LAYERS, R, 128), f32), vmem((4, R // 2, 128), f32),
            vmem((4, R, 128), f32), vmem((R, 128), f32), vmem((NZ, ZR, 128), f32), vmem((NZ, ZR, 128), f32),
            vmem((ZR, 128), f32), vmem((NY, ZR, 128), f32), vmem((2, NZ, ZR, 128), f32),
            dma((6, 2, 8)), dma((2, NY)),
        ]

    def to(self, src, dst, phase, i, dp, own):
        return remote(src, dst, self.sems.at[phase, 0, i], self.sems.at[phase, 1, i], dp, own)

    def x_peer(self, d):
        return self.yl * 4 + lax.rem(self.x + d, 4)

    def yl_peer(self):
        return (1 - self.yl) * 4 + self.x

    def layer_of(self, t):
        return (self.yl if t % 2 else 1 - self.yl) * 4 + lax.rem(self.x + DX[t], 4)

    def z_peer(self, i):
        zz = lax.rem(self.z + i, NZ)
        return zz, zz * 8 + self.yh * 2 + self.core

    def y_peer(self, i):
        return self.z * 8 + lax.rem(self.yh + i, NY) * 2 + self.core

    def mine(self, t):
        return self.part.at[t, self.core]

    def core_copy(self, t):
        return self.to(self.part.at[t, 1 - self.core], self.core_rx.at[t], 0, t, self.sib, self.own)

    def relay(self, i):
        half = pl.ds(0, R // 2) if i < 2 else pl.ds(R // 2, R // 2)
        return self.to(
            self.part.at[i % 2, self.core, half], self.relay_rx.at[i], 1, i, self.dp, self.x_peer(1 if i < 2 else 3)
        )

    def x_copy(self, i):
        return self.to(self.mine(i + 2), self.x_rx.at[i], 2, i, self.dp, self.x_peer(1 if i < 2 else 3))

    def yl_copy(self):
        return self.to(self.mine(6), self.yl_rx, 2, 4, self.dp, self.yl_peer())

    def pass_on(self, t):
        self.core_copy(t).wait_recv()
        total = self.part[t, self.core] + self.core_rx[t]
        if t < 2:
            self.part[t, self.core] = total
            self.relay(t).start()
            self.relay(t + 2).start()
        elif t < 6:
            i = t - 2
            self.relay(i).wait_recv()
            lo = 0 if i < 2 else R // 2
            self.part[t, self.core] = total
            self.part[t, self.core, lo : lo + R // 2] = total[lo : lo + R // 2] + self.relay_rx[i]
            self.x_copy(i).start()
        else:
            self.part[t, self.core] = total

    def x_sum(self, t):
        total = self.part[t, self.core]
        for i in (t - 6, t - 4):
            self.x_copy(i).wait_recv()
            total = total + self.x_rx[i]
        return total

    def x_done(self):
        self.part[6, self.core] = self.x_sum(6)
        self.yl_copy().start()
        self.part[7, self.core] = self.x_sum(7)

    def yl_done(self):
        self.yl_copy().wait_recv()
        total = self.part[7, self.core] + self.yl_rx[...]
        self.z_tx[...] = total.reshape(NZ, ZR, 128)
        for i in (4, 3, 5, 2, 6, 1, 7):
            self.z_copy(i).start()

    def z_copy(self, i):
        zz, peer = self.z_peer(i)
        return self.to(self.z_tx.at[zz], self.z_rx.at[i], 3, i, peer, self.own)

    def y_copy(self, i):
        return remote(self.y_tx, self.y_rx.at[i], self.sems_y.at[0, i], self.sems_y.at[1, i], self.y_peer(i), self.own)

    def z_done(self):
        acc = self.z_tx[self.z]
        for i in range(1, NZ):
            self.z_copy(i).wait_recv()
            acc = acc + self.z_rx[i]
        self.y_tx[...] = acc
        for i in (2, 1, 3):
            self.y_copy(i).start()

    def gather_copy(self, i):
        block = self.fin.at[self.core, self.z]
        return self.to(block, block, 4, i, self.z_peer(i)[1], self.own)

    def from_z(self, core, i):
        return self.fin.at[core, lax.rem(self.z + NZ - i, NZ)]

    def arrival(self, i):
        block = self.from_z(self.core, i)
        return self.to(block, block, 4, i, self.z_peer(i)[1], self.own)

    def twin_copy(self, i):
        block = self.from_z(self.core, i)
        return self.to(block, block, 5, i, self.sib, self.own)

    def twin_arrival(self, i):
        block = self.from_z(1 - self.core, i)
        return self.to(block, block, 5, i, self.sib, self.own)

    def y_done(self):
        acc = self.y_tx[...]
        for i in range(1, NY):
            self.y_copy(i).wait_recv()
            acc = acc + self.y_rx[i]
        self.fin[self.core, self.z] = acc
        for i in (4, 3, 5, 2, 6, 1, 7):
            self.gather_copy(i).start()
        self.twin_copy(0).start()

    def gather_done(self):
        for i in (1, 7, 2, 6, 3, 5, 4):
            self.arrival(i).wait_recv()
            self.twin_copy(i).start()

    def twin_done(self):
        for i in range(NZ):
            self.twin_arrival(i).wait_recv()

    def drain(self):
        for t in range(LAYERS):
            self.core_copy(t).wait_send()
        for i in range(4):
            self.relay(i).wait_send()
            self.x_copy(i).wait_send()
        self.yl_copy().wait_send()
        for i in range(1, NZ):
            self.z_copy(i).wait_send()
            self.gather_copy(i).wait_send()
        for i in range(1, NY):
            self.y_copy(i).wait_send()
        for i in range(NZ):
            self.twin_copy(i).wait_send()


def split3(x):
    a = x.astype(bf16)
    r = x - a.astype(f32)
    b = r.astype(bf16)
    r = r - b.astype(f32)
    return a, b, r.astype(bf16)


def outer(p, r):
    p1, p2, p3 = split3(p)
    r1, r2, r3 = split3(r)
    lhs = jnp.concatenate([p1, p1, p2, p2, p1, p3], 0)
    rhs = jnp.concatenate([r1, r2, r1, r2, r3, r1], 0)
    return lax.dot_general(lhs, rhs, (((0,), (0,)), ((), ())), preferred_element_type=f32)


class Sweep:
    def __init__(self, ref, n):
        self.ref, self.n, self.ahead = ref, n, None

    def load(self, k):
        rows = self.ref[8 * k : 8 * k + 8, :]
        return [rows[:, 128 * c : 128 * c + 128] for c in range(self.n // 128)]

    def panel(self, k):
        lo, n = 8 * k, self.n
        kc, kl = lo // 128, lo % 128
        sub = lax.broadcasted_iota(jnp.int32, (8, 128), 0)
        lane = lax.broadcasted_iota(jnp.int32, (8, 128), 1)
        chunks = self.load(k) if self.ahead is None else self.ahead
        rows = jnp.concatenate(chunks, 1) if n > 128 else chunks[0]

        def column(x, j):
            return jnp.broadcast_to(x[:, j : j + 1], (8, 128))

        def row(x, j):
            return jnp.broadcast_to(x[j : j + 1, :], (8, 128))

        cols = [column(chunks[kc], kl + j) for j in range(8)]
        more = lo + 8 < n
        if more:
            raw = self.load(k + 1)
            weights = [column(raw[kc], kl + m) for m in range(8)]
        for p in range(8):
            rec = 1.0 / row(cols[p], p)
            factor = cols[p]
            here = sub == p
            chunks = list(chunks)
            chunks[kc] = jnp.where(lane == kl + p, jnp.where(here, 1.0, 0.0), chunks[kc])

            def step(x):
                scaled = row(x, p) * rec
                return jnp.where(here, scaled, x - factor * scaled)

            cols = [step(cols[j]) if j > p else cols[j] for j in range(8)]
            chunks = [step(x) for x in chunks]
        inside = (lane >= kl) & (lane < kl + 8)
        chunks[kc] = jnp.where(inside, -chunks[kc], chunks[kc])
        swept = jnp.concatenate(chunks, 1) if n > 128 else chunks[0]
        if more:
            self.ahead = []
            for c in range(n // 128):
                old = jnp.where(inside, 0.0, raw[c]) if c == kc else raw[c]
                t = [weights[m] * row(chunks[c], m) for m in range(8)]
                self.ahead.append(old - (((t[0] + t[1]) + (t[2] + t[3])) + ((t[4] + t[5]) + (t[6] + t[7]))))
        change = outer(rows, swept)
        lanes = lax.broadcasted_iota(jnp.int32, (1, n), 1)
        own_cols = (lanes >= lo) & (lanes < lo + 8)
        self.ref[...] = jnp.where(own_cols, 0.0, self.ref[...]) - change
        self.ref[lo : lo + 8, :] = swept


def eye(n):
    i = lax.broadcasted_iota(jnp.int32, (n, n), 0)
    j = lax.broadcasted_iota(jnp.int32, (n, n), 1)
    return jnp.where(i == j, 1.0, 0.0).astype(f32)


def main_kernel(scale, wide_hbm, narrow_hbm, out_ref, wbuf, nbuf, in_sem, a_ref, n_ref, cols_ref, x_sem, *refs):
    first, second = Stream(refs[:12]), Stream(refs[12:])
    dp, own, z, yh, core = place()

    def loads(t):
        l = first.layer_of(t)
        return (
            pltpu.make_async_copy(wide_hbm.at[l], wbuf.at[t], in_sem.at[0, t]),
            pltpu.make_async_copy(narrow_hbm.at[l], nbuf.at[t], in_sem.at[1, t]),
        )

    for part in range(2):
        for t in range(LAYERS):
            loads(t)[part].start()

    def own_peer(i):
        return lax.rem(own + i, NO)

    barrier = pltpu.get_barrier_semaphore()

    def greet(dp, own):
        pl.semaphore_signal(barrier, inc=1, device_id=(dp, own), device_id_type=MESH)

    greet(first.sib, own)
    for i in range(1, NO):
        greet(dp, own_peer(i))
    for i in range(1, NZ):
        greet(first.z_peer(i)[1], own)
    for i in range(1, NY):
        greet(first.y_peer(i), own)

    def stats_first(t):
        loads(t)[0].wait()
        wide = wbuf[t]
        right = wide[:, 128:]
        top = gram(wide[:, :128], wide)
        first.part[t, 0, 0:128, :] = top[:, :128]
        first.part[t, 0, 128:192, :] = top[0:64, 128:]
        first.part[t, 1, 0:64, :] = top[64:128, 128:]
        first.part[t, 1, 64:192, :] = gram(right, right)

    def stats_second(t):
        loads(t)[1].wait()
        narrow = nbuf[t]
        mixed = gram(narrow, wbuf[t])
        second.part[t, 0, 0:128, :] = gram(narrow, narrow)
        second.part[t, 0, 128:192, :] = mixed[0:64, :128]
        second.part[t, 1, 0:64, :] = mixed[64:128, :128]
        second.part[t, 1, 64:192, :] = mixed[:, 128:]

    stats_first(0)
    pl.semaphore_wait(barrier, 1 + (NO - 1) + (NZ - 1) + (NY - 1))
    first.core_copy(0).start()
    for t in range(1, LAYERS):
        stats_first(t)
        first.core_copy(t).start()
        if t >= LAG:
            first.pass_on(t - LAG)
    for t in range(LAYERS):
        stats_second(t)
        second.core_copy(t).start()
        if t < LAG:
            first.pass_on(LAYERS - LAG + t)
        else:
            second.pass_on(t - LAG)
    for t in range(LAYERS - LAG, LAYERS):
        second.pass_on(t)
    first.x_done()
    first.yl_done()
    second.x_done()
    second.yl_done()
    first.z_done()
    second.z_done()
    first.y_done()
    first.gather_done()
    first.twin_done()
    second.y_done()

    damp = DAMP * eye(128)
    wide = first.fin[...].reshape(384, 128) * scale
    cross = wide[128:256]
    a_ref[0:128, 0:128] = wide[0:128] + damp
    a_ref[0:128, 128:256] = cross
    a_ref[128:256, 0:128] = cross.T
    a_ref[128:256, 128:256] = wide[256:384] + damp
    a_sweep, n_sweep = Sweep(a_ref, WIDE), Sweep(n_ref, NARROW)
    late = (WIDE - NARROW) // 8
    for k in range(WIDE // 8):
        a_sweep.panel(k)
        if k == late - 2:
            second.gather_done()
        if k == late - 1:
            second.twin_done()
            n_ref[...] = second.fin[...].reshape(384, 128)[0:128] * scale + damp
        if k >= late:
            n_sweep.panel(k - late)
    x = -a_ref[pl.ds(pl.multiple_of(dp // 2 * 8, 8), 8), :]
    last = (((1,), (1,)), ((), ()))
    mixed = second.fin[...].reshape(384, 128)[128:384] * scale
    inner = 0.0
    for b in range(2):
        half = mixed[128 * b : 128 * b + 128]
        inner = inner + lax.dot_general(x[:, 128 * b : 128 * b + 128], half, last, precision=HI, preferred_element_type=f32)
    u = -jnp.dot(inner, n_ref[...], precision=HI, preferred_element_type=f32)
    both = jnp.concatenate([x, u], 1)
    cols_ref[...] = jnp.where(core == 0, both[0:4], both[4:8])

    def copy(i):
        return remote(cols_ref, out_ref.at[own], x_sem.at[0, i], x_sem.at[1, i], dp, own_peer(i))

    def arrival(i):
        return remote(cols_ref, out_ref.at[own_peer(NO - i)], x_sem.at[0, i], x_sem.at[1, i], dp, own_peer(i))

    for i in (6, 2, 5, 7, 1, 3, 4):
        copy(i).start()
    out_ref[own] = cols_ref[...]
    first.drain()
    second.drain()
    for i in range(1, NO):
        arrival(i).wait_recv()
    for i in range(1, NO):
        copy(i).wait_send()


def columns(wide_rows, narrow_rows, total):
    vmem, dma = pltpu.VMEM, pltpu.SemaphoreType.DMA
    return pl.pallas_call(
        functools.partial(main_kernel, 1.0 / total),
        out_shape=jax.ShapeDtypeStruct((NO, 4, WIDE + NARROW), f32),
        in_specs=[pl.BlockSpec(memory_space=pltpu.HBM)] * 2,
        out_specs=pl.BlockSpec(memory_space=pltpu.VMEM),
        scratch_shapes=[
            vmem((LAYERS, ROWS, WIDE), bf16), vmem((LAYERS, ROWS, NARROW), bf16), dma((2, LAYERS)),
            vmem((WIDE, WIDE), f32), vmem((NARROW, NARROW), f32), vmem((4, WIDE + NARROW), f32), dma((2, NO)),
            *Stream.scratch(), *Stream.scratch(),
        ],
        compiler_params=pltpu.CompilerParams(
            collective_id=0, has_side_effects=True, vmem_limit_bytes=60 << 20
        ),
    )(wide_rows, narrow_rows)


def select_kernel(owners, cols_ref, kept_ref, update_ref):
    dp, own, _, _, _ = place()
    i0 = lax.broadcasted_iota(jnp.int32, (4, WIDE), 0)
    i1 = lax.broadcasted_iota(jnp.int32, (4, WIDE), 1)
    empty = jnp.where(i1 == dp * 4 + i0, 1.0 / DAMP, 0.0).astype(f32)
    kept = [empty, empty]
    shift = lax.rem(128 - 16 * own, 128)
    for l in range(LAYERS):
        slot = owners[l] * 2
        for j in range(l):
            slot = slot + jnp.where(owners[j] == owners[l], 1, 0)
        got = cols_ref[l]
        kept = [jnp.where(slot == own * 2 + c, got[:, :WIDE], kept[c]) for c in range(2)]
        part = jnp.concatenate([got[:, WIDE:], got[:, WIDE:]], 0)
        update_ref[l] = pltpu.roll(part, shift, 1)[0:4, 0:16]
    kept_ref[0] = kept[0]
    kept_ref[1] = kept[1]


def select(owner_map, cols):
    vmem = pl.BlockSpec(memory_space=pltpu.VMEM)
    return pl.pallas_call(
        select_kernel,
        out_shape=(
            jax.ShapeDtypeStruct((2, 4, WIDE), f32),
            jax.ShapeDtypeStruct((LAYERS, 4, 16), f32),
        ),
        in_specs=[pl.BlockSpec(memory_space=pltpu.SMEM), vmem],
        out_specs=(vmem, vmem),
    )(owner_map, cols)


def on_device(wide_rows, narrow_rows, owner_map):
    cols = columns(wide_rows, narrow_rows, ROWS * 512)
    kept, update = select(owner_map, cols)
    return kept.transpose(0, 2, 1), update.transpose(0, 2, 1)


def solution(mesh):
    in_specs = (P(None, ("dp", "own"), None), P(None, ("dp", "own"), None), P())
    out_specs = (P("own", None, "dp"), P(None, "own", "dp"))
    return jax.shard_map(
        on_device, mesh=mesh, in_specs=in_specs, out_specs=out_specs, check_vma=False
    )
```
